32 devices in a mesh: rep: 4 (over x, core), shard: 8 (over z, y).
Axes of the slice: x: 2, y: 2, z: 4, core: 2. Of those that a mesh axis runs over, the one named last changes fastest.
Arguments:
- tokens: bfloat16 [8192, 1024], P(('rep', 'shard')), may hold values from -6 to 6
- norm_attn: bfloat16 [1024], P('shard'), may hold values from 0.099609375 to 1.8984375
- w_query: bfloat16 [1024, 1024], P('shard'), may hold values from -0.375 to 0.375
- w_latent: bfloat16 [1024, 512], P('shard'), may hold values from -0.1875 to 0.1875
- w_key_up: bfloat16 [2, 256, 512], P(None, 'shard'), may hold values from -0.375 to 0.375
- w_value_up: bfloat16 [2, 256, 512], P(None, 'shard'), may hold values from -0.375 to 0.375
- w_out: bfloat16 [1024, 1024], P(None, 'shard'), may hold values from -0.75 to 0.75
- norm_ffn: bfloat16 [1024], P('shard'), may hold values from 0.099609375 to 1.8984375
- w_gate: bfloat16 [1024, 2816], P('shard'), may hold values from -0.1875 to 0.1875
- w_up: bfloat16 [1024, 2816], P('shard'), may hold values from -0.1875 to 0.1875
- w_down: bfloat16 [2816, 1024], P('shard'), may hold values from -0.109375 to 0.109375
- cotangent: bfloat16 [8192, 1024], P(('rep', 'shard')), may hold values from -6 to 6
Outputs:
- output: bfloat16 [8192, 1024], P(('rep', 'shard'))
- grad_tokens: bfloat16 [8192, 1024], P(('rep', 'shard'))
- grad_norm_attn: float32 [1024], P('shard')
- grad_w_query: float32 [1024, 1024], P('shard')
- grad_w_latent: float32 [1024, 512], P('shard')
- grad_w_key_up: float32 [2, 256, 512], P(None, 'shard')
- grad_w_value_up: float32 [2, 256, 512], P(None, 'shard')
- grad_w_out: float32 [1024, 1024], P(None, 'shard')
- grad_norm_ffn: float32 [1024], P('shard')
- grad_w_gate: float32 [1024, 2816], P('shard')
- grad_w_up: float32 [1024, 2816], P('shard')
- grad_w_down: float32 [2816, 1024], P('shard')
The draws below stay inside these ranges and needn't reach their ends.
All inputs are finite; a program needn't handle non-finite values.
Results may differ from the reference program's by a relative error of at most 0.018.
Values may be sent and summed in bfloat16 or wider, within the bound.
No kernel may reach another device: no remote copies, remote signals or barrier semaphores. Data moves between devices by JAX's collectives and lax.ppermute only.
A program may use at most 192 MiB of HBM per device.

```python
import math
import jax
import jax.numpy as jnp
from jax import lax

D = 1024
HQ = 16
HD = 64
LG = 2
LAT = 256
FF = 2816
SEQ_LEN = 256
TOKENS = 8192


def with_spikes(entries, key, source, target, blocks, factor):
    owner, partner = [(jnp.arange(entries.shape[dim]) // (entries.shape[dim] // blocks)).reshape([-1 if axis == dim else 1 for axis in range(entries.ndim)]) for dim in (source, target)]
    chosen = jax.random.permutation(key, blocks)[partner]
    strong = (owner == chosen) | (owner == (partner + blocks // 2) % blocks)
    return jnp.where(strong, factor * entries, entries)


def block_levels(stream_key, shape, cuts, low, high):
    loudness = 1.0
    for axis_at, blocks in cuts:
        heights = jax.random.uniform(jax.random.fold_in(jax.random.fold_in(stream_key, 6), axis_at), (blocks,), jnp.float32, low / len(cuts), high / len(cuts))
        loudness = loudness * jnp.repeat(jnp.exp(heights), shape[axis_at] // blocks).reshape((-1,) + (1,) * (len(shape) - 1 - axis_at))
    return loudness


def centred(key, dims, deviation, limit, pieces=(), dtype=jnp.bfloat16):
    gain = block_levels(key, dims, pieces, -0.22, 0.18) if pieces else 1.0
    values = jax.random.normal(key, dims, jnp.float32) * deviation * gain
    return jnp.minimum(jnp.maximum(values, -limit), limit).astype(dtype)


def gaussian_with(own_key, dims, scale, reach, pieces, heavy, dtype=jnp.bfloat16):
    array = scale * jax.random.normal(own_key, dims, jnp.float32)
    if pieces:
        array = array * block_levels(own_key, dims, pieces, -0.22, 0.18)
    return jnp.clip(with_spikes(array, jax.random.fold_in(own_key, 3), *heavy), -reach, reach).astype(dtype)


def setup_inputs(seed: int = 0) -> dict:
    splits = jax.random.split(jax.random.key(seed), 13)
    return {
        "tokens": centred(splits[0], (TOKENS, D), 1.0, 6.0, ((0, 32),)),
        "norm_attn": jnp.clip(1.0 + 0.18 * jax.random.normal(splits[1], (D,), jnp.float32), 0.099609375, 1.8984375).astype(jnp.bfloat16),
        "w_query": centred(splits[2], (D, HQ * HD), (D // 4) ** -0.5, 0.375, ((0, 8),)),
        "w_latent": centred(splits[3], (D, LG * LAT), D ** -0.5, 0.1875, ((0, 8),)),
        "w_key_up": centred(splits[4], (LG, LAT, HQ * HD // LG), LAT ** -0.5, 0.375, ((1, 8),)),
        "w_value_up": centred(splits[5], (LG, LAT, HQ * HD // LG), LAT ** -0.5, 0.375, ((1, 8),)),
        "w_out": centred(splits[6], (HQ * HD, D), (HQ * HD // 16) ** -0.5, 0.75, ((1, 8),)),
        "norm_ffn": jnp.clip(1.0 + 0.18 * jax.random.normal(splits[7], (D,), jnp.float32), 0.099609375, 1.8984375).astype(jnp.bfloat16),
        "w_gate": centred(splits[8], (D, FF), D ** -0.5, 0.1875, ((0, 8),)),
        "w_up": centred(splits[9], (D, FF), D ** -0.5, 0.1875, ((0, 8),)),
        "w_down": centred(splits[10], (FF, D), FF ** -0.5, 0.109375, ((0, 8),)),
        "cotangent": gaussian_with(splits[11], (TOKENS, D), 1.0, 6.0, ((0, 32),), (0, 1, 32, 2.75)),
    }


@jax.custom_vjp
def low(v):
    return lax.optimization_barrier(v.astype(jnp.bfloat16)).astype(jnp.float32)

@jax.custom_vjp
def low_back(v):
    return v

def low_keep(v):
    return (low(v), None)

def low_pass(kept, grad):
    return (grad,)

def back_keep(v):
    return (v, None)

def back_low(kept, grad):
    return (low(grad),)
low.defvjp(low_keep, low_pass)
low_back.defvjp(back_keep, back_low)
epsilon = 1e-05
highest = lax.Precision.HIGHEST

def rms_scale(rows_in):
    return lax.rsqrt(lax.optimization_barrier(jnp.mean(rows_in * rows_in, axis=-1, keepdims=True)) + epsilon)

def attention(queries, latents, w_key_up, w_value_up):
    length = queries.shape[0]
    grouped = latents.reshape(length, LG, LAT)
    key_heads = low_back(low(jnp.einsum('tgl,glk->tgk', grouped, w_key_up, precision=highest))).reshape(length, HQ, HD)
    value_heads = low_back(low(jnp.einsum('tgl,glk->tgk', grouped, w_value_up, precision=highest))).reshape(length, HQ, HD)
    query_heads = queries.reshape(length, HQ, HD)
    scores = low_back(jnp.einsum('qhd,khd->hqk', query_heads, key_heads, precision=highest) * HD ** (-0.5))
    row_ids = lax.broadcasted_iota(jnp.int32, (length, length), 0)
    col_ids = lax.broadcasted_iota(jnp.int32, (length, length), 1)
    scores = jnp.where(col_ids <= row_ids, scores, -1e+30)
    attn_probs = jax.nn.softmax(scores, axis=-1)
    mixed_heads = jnp.einsum('hqk,khd->qhd', low(attn_probs), value_heads, precision=highest)
    return mixed_heads.reshape(length, HQ * HD)

def layer_block(rows_in, params):
    norm_attn, w_query, w_latent, w_key_up, w_value_up, w_out, norm_ffn, w_gate, w_up, w_down = params
    normed_attn = low(rows_in * rms_scale(rows_in) * norm_attn)
    queries = low_back(low(jnp.dot(normed_attn, w_query, precision=highest)))
    latents = low_back(low(jnp.dot(normed_attn, w_latent, precision=highest)))
    seq_count = rows_in.shape[0] // SEQ_LEN
    mixed_heads = jax.vmap(attention, in_axes=(0, 0, None, None))(queries.reshape(seq_count, SEQ_LEN, HQ * HD), latents.reshape(seq_count, SEQ_LEN, LG * LAT), w_key_up, w_value_up)
    mixed_heads = low_back(low(mixed_heads.reshape(rows_in.shape[0], HQ * HD)))
    attn_out = low_back(jnp.dot(mixed_heads, w_out, precision=highest))
    residual = rows_in + attn_out
    normed_ffn = low(residual * rms_scale(residual) * norm_ffn)
    gate_proj = low_back(jnp.dot(normed_ffn, w_gate, precision=highest))
    up_proj = low_back(jnp.dot(normed_ffn, w_up, precision=highest))
    activated = low(jax.nn.silu(gate_proj) * up_proj)
    ffn_out = low_back(jnp.dot(activated, w_down, precision=highest))
    return residual + ffn_out

def layer(inputs, params):
    seq_total = TOKENS // SEQ_LEN
    per_block = math.gcd(seq_total, max(1, 4096 // SEQ_LEN))
    block_count = seq_total // per_block
    blocks = inputs.reshape(block_count, per_block * SEQ_LEN, D)
    results = lax.map(jax.checkpoint(lambda block_rows: layer_block(block_rows, params)), blocks)
    return results.reshape(TOKENS, D)

def reference(tokens, norm_attn, w_query, w_latent, w_key_up, w_value_up, w_out, norm_ffn, w_gate, w_up, w_down, cotangent):
    params = tuple((item.astype(jnp.float32) for item in (norm_attn, w_query, w_latent, w_key_up, w_value_up, w_out, norm_ffn, w_gate, w_up, w_down)))
    inputs = tokens.astype(jnp.float32)
    result, pullback = jax.vjp(layer, inputs, params)
    grad_inputs, grad_params = pullback(cotangent.astype(jnp.float32))
    return (result.astype(jnp.bfloat16), grad_inputs.astype(jnp.bfloat16), grad_params[0], grad_params[1], grad_params[2], grad_params[3], grad_params[4], grad_params[5], grad_params[6], grad_params[7], grad_params[8], grad_params[9])
```

```python
import jax
import jax.numpy as jnp
from jax import lax
from jax.sharding import PartitionSpec as P

HQ = 16
HD = 64
LG = 2
LAT = 256
SEQ = 256

epsilon = 1e-05
f32 = jnp.float32
bf16 = jnp.bfloat16


def radices(count):
    bits = count.bit_length() - 1
    top = 1
    while top * (top + 1) // 2 < bits:
        top += 1
    out = []
    while bits > 0:
        take = min(top, bits)
        out.append(2**take)
        bits -= take
        top = max(1, top - 1)
    return out or [1]


def rms_scale(rows_in):
    return lax.rsqrt(jnp.mean(rows_in * rows_in, axis=-1, keepdims=True) + epsilon)


def dot(left, right):
    return jnp.dot(left, right, preferred_element_type=f32)


def dot_tn(left, right):
    return lax.dot_general(left, right, (((0,), (0,)), ((), ())), preferred_element_type=f32)


def dot_nt(left, right):
    return lax.dot_general(left, right, (((1,), (1,)), ((), ())), preferred_element_type=f32)


class Net:
    def __init__(self, rep_count, shard_count):
        self.R = rep_count
        self.S = shard_count
        self.radix = radices(shard_count)
        self.stride = []
        acc = shard_count
        for radix in self.radix:
            acc //= radix
            self.stride.append(acc)

    def flip(self, value, mask):
        return lax.ppermute(value, "rep", [(i, i ^ mask) for i in range(self.R)])

    def digit_of(self, index, axis):
        return (index // self.stride[axis]) % self.radix[axis]

    def moved(self, index, axis, by):
        radix, stride = self.radix[axis], self.stride[axis]
        digit = (index // stride) % radix
        return index + ((digit + by) % radix - digit) * stride

    def shift(self, value, axis, by):
        pairs = [(i, self.moved(i, axis, by)) for i in range(self.S)]
        return lax.ppermute(value, "shard", pairs)

    def gather_blocks(self, block, me, after=None):
        first = []
        blocks = [((), block)]
        for axis, radix in enumerate(self.radix):
            new = list(blocks)
            for moves, value in blocks:
                for by in range(1, radix):
                    source = value
                    if axis == 0 and after is not None:
                        source, _ = lax.optimization_barrier((value, after[by - 1]))
                    arrived = self.shift(source, axis, by)
                    if axis == 0:
                        first.append(arrived)
                    new.append((moves + ((axis, by),), arrived))
            blocks = new
        out = []
        for moves, value in blocks:
            source = me
            for axis, by in moves:
                source = self.moved(source, axis, -by)
            out.append((source, value))
        return out, first

    def place(self, blocks, rows):
        shape = blocks[0][1].shape
        full = jnp.zeros((self.S * rows,) + shape[1:], blocks[0][1].dtype)
        for source, value in blocks:
            start = (source * rows,) + (0,) * (len(shape) - 1)
            full = lax.dynamic_update_slice(full, value, start)
        return full

    def scatter_sum(self, blocks, me):
        tail = blocks.shape[1:]
        value = blocks.astype(bf16)
        for axis in reversed(range(len(self.radix))):
            radix = self.radix[axis]
            value = value.reshape((-1, radix) + tail)
            digit = self.digit_of(me, axis)
            pick = lambda by: lax.dynamic_index_in_dim(value, (digit + by) % radix, 1, False)
            total = pick(0).astype(f32)
            for by in range(1, radix):
                total = total + self.shift(pick(by), axis, by).astype(f32)
            value = total.astype(bf16) if axis else total
        return value.reshape(tail)

    def rep_gather(self, value):
        blocks = {0: value}
        bit = self.R >> 1
        while bit:
            for j in list(blocks):
                blocks[j ^ bit] = self.flip(blocks[j], bit)
            bit >>= 1
        return [blocks[j] for j in range(self.R)]

    def rep_scatter(self, value):
        tail = value.shape[1:]
        bit = 1
        while bit < self.R:
            value = value.reshape((-1, 2) + tail)
            value = value[:, 0].astype(f32) + self.flip(value[:, 1].astype(bf16), bit).astype(f32)
            bit <<= 1
        return value.reshape(tail)


def attention(queries, keys, values):
    scores = jnp.einsum("shqd,shkd->shqk", queries, keys, preferred_element_type=f32) * HD ** (-0.5)
    length = queries.shape[2]
    row_ids = lax.broadcasted_iota(jnp.int32, (length, length), 0)
    col_ids = lax.broadcasted_iota(jnp.int32, (length, length), 1)
    return jnp.where(col_ids <= row_ids, scores, -1e30)


def shards(net, tokens, norm_attn, w_query, w_latent, w_key_up, w_value_up, w_out, norm_ffn,
           w_gate, w_up, w_down, cotangent):
    R, S = net.R, net.S
    rep = lax.axis_index("rep")
    me = lax.axis_index("shard")
    core = rep % 2
    rows, D = tokens.shape
    part = D // S
    heads = HQ // 2
    wide = heads * HD
    FF = w_gate.shape[1]
    sub = FF // (S * R)
    mine = sub * S
    lat_rows = LAT // S

    def half(value, axis):
        size = value.shape[axis] // 2
        return lax.dynamic_slice_in_dim(value, core * size, size, axis)

    piece_a = jnp.concatenate([half(w_query, 1), half(w_latent, 1), half(w_out, 0).T], axis=1)
    gains = jnp.stack([norm_attn, norm_ffn])
    gains = jnp.pad(gains, ((0, 14), (0, wide - part)))
    piece_k = jnp.concatenate([half(w_key_up, 0)[0], half(w_value_up, 0)[0], gains], axis=0)

    def columns(weight):
        split = weight.reshape(weight.shape[0], S, R, sub)
        return lax.dynamic_index_in_dim(split, rep, 2, False).reshape(weight.shape[0], mine)

    piece_g = jnp.stack([columns(w_gate), columns(w_up)], axis=1)
    piece_d = lax.dynamic_slice_in_dim(w_down, rep * sub, sub, 0)

    tokens_b = net.flip(tokens, 1)
    blocks_a, first_a = net.gather_blocks(piece_a, me)
    blocks_k, _ = net.gather_blocks(piece_k, me)
    blocks_g, first_g = net.gather_blocks(piece_g, me, first_a)
    blocks_d, first_d = net.gather_blocks(piece_d, me, first_g)
    full_a = net.place(blocks_a, part)
    query_full = full_a[:, :wide]
    latent_full = full_a[:, wide : wide + LAT]
    out_t = full_a[:, wide + LAT :]
    key_full = net.place([(s, v[:lat_rows]) for s, v in blocks_k], lat_rows)
    value_full = net.place([(s, v[lat_rows : 2 * lat_rows]) for s, v in blocks_k], lat_rows)
    gain_rows = net.place([(s, v[None, 2 * lat_rows : 2 * lat_rows + 2, :part]) for s, v in blocks_k], 1)
    gain_rows = gain_rows.astype(f32).transpose(1, 0, 2).reshape(2, D)
    gain_attn, gain_ffn = gain_rows[0], gain_rows[1]
    full_g = net.place(blocks_g, part)
    gate_full, up_full = full_g[:, 0], full_g[:, 1]
    down_full = net.place(blocks_d, sub)

    pair = jnp.concatenate([tokens, tokens_b], axis=0)
    inputs = pair.astype(f32)
    scale_attn = rms_scale(inputs)
    normed_attn = (inputs * scale_attn * gain_attn).astype(bf16)
    queries = dot(normed_attn, query_full).astype(bf16)
    latents = dot(normed_attn, latent_full).astype(bf16)
    keys = dot(latents, key_full).astype(bf16)
    values = dot(latents, value_full).astype(bf16)

    def split_heads(value):
        return value.reshape(-1, SEQ, heads, HD).transpose(0, 2, 1, 3)

    def join_heads(value):
        return value.transpose(0, 2, 1, 3).reshape(2 * rows, wide)

    q_heads, k_heads, v_heads = split_heads(queries), split_heads(keys), split_heads(values)
    scores = attention(q_heads, k_heads, v_heads)
    maxima = jnp.max(scores, axis=-1, keepdims=True)
    log_total = maxima + jnp.log(jnp.sum(jnp.exp(scores - maxima), axis=-1, keepdims=True))
    probs = jnp.exp(scores - log_total)
    probs_low = probs.astype(bf16)
    mixed = jnp.einsum("shqk,shkd->shqd", probs_low, v_heads, preferred_element_type=f32)
    mixed = join_heads(mixed.astype(bf16))
    attn_part = dot_nt(mixed, out_t)
    residual = inputs[:rows] + attn_part[:rows] + net.flip(attn_part[rows:], 1)

    scale_ffn = rms_scale(residual)
    normed_own = (residual * scale_ffn * gain_ffn).astype(bf16)
    normed_ffn = jnp.concatenate(net.rep_gather(normed_own), axis=0)
    cots = jnp.concatenate(net.rep_gather(cotangent), axis=0)
    gate_proj = dot(normed_ffn, gate_full)
    up_proj = dot(normed_ffn, up_full)
    sigmoid_gate = jax.nn.sigmoid(gate_proj)
    silu_gate = gate_proj * sigmoid_gate
    activated = (silu_gate * up_proj).astype(bf16)
    grad_down = dot_tn(activated, cots)
    sum_down = net.scatter_sum(grad_down.reshape(S, sub, D), me)
    grad_act = dot_nt(cots, down_full)
    grad_gate = (
        grad_act * up_proj * sigmoid_gate * (1.0 + gate_proj * (1.0 - sigmoid_gate))
    ).astype(bf16)
    grad_up = (grad_act * silu_gate).astype(bf16)
    grad_gate_w = dot_tn(normed_ffn, grad_gate)
    grad_up_w = dot_tn(normed_ffn, grad_up)
    sum_gate = net.scatter_sum(grad_gate_w.reshape(S, part, mine), me)
    sum_up = net.scatter_sum(grad_up_w.reshape(S, part, mine), me)
    grad_normed = dot_nt(grad_gate, gate_full) + dot_nt(grad_up, up_full)
    grad_normed = net.rep_scatter(grad_normed.reshape(R, rows, D))
    down_out = net.rep_scatter(dot(activated, down_full).reshape(R, rows, D))
    output = (residual + down_out).astype(bf16)
    grad_norm_ffn = jnp.sum(grad_normed * residual * scale_ffn, axis=0)
    weighted = grad_normed * gain_ffn
    grad_residual = (
        cotangent.astype(f32)
        + scale_ffn * weighted
        - residual * scale_ffn**3 * jnp.mean(weighted * residual, axis=-1, keepdims=True)
    )

    grad_attn_own = grad_residual.astype(bf16)
    grad_attn = jnp.concatenate([grad_attn_own, net.flip(grad_attn_own, 1)], axis=0)
    grad_out_t = dot_tn(grad_attn, mixed)
    grad_mixed = split_heads(dot(grad_attn, out_t).astype(bf16))
    grad_probs = jnp.einsum("shqd,shkd->shqk", grad_mixed, v_heads, preferred_element_type=f32)
    grad_scores = (
        probs * (grad_probs - jnp.sum(probs * grad_probs, axis=-1, keepdims=True))
    ).astype(bf16)
    grad_q = jnp.einsum("shqk,shkd->shqd", grad_scores, k_heads, preferred_element_type=f32)
    grad_k = jnp.einsum("shqk,shqd->shkd", grad_scores, q_heads, preferred_element_type=f32)
    grad_v = jnp.einsum("shqk,shqd->shkd", probs_low, grad_mixed, preferred_element_type=f32)
    grad_q = join_heads((grad_q * HD ** (-0.5)).astype(bf16))
    grad_k = join_heads((grad_k * HD ** (-0.5)).astype(bf16))
    grad_v = join_heads(grad_v.astype(bf16))
    grad_key_up = dot_tn(latents, grad_k)
    grad_value_up = dot_tn(latents, grad_v)
    grad_lat = (dot_nt(grad_k, key_full) + dot_nt(grad_v, value_full)).astype(bf16)
    grad_query_w = dot_tn(normed_attn, grad_q)
    grad_latent_w = dot_tn(normed_attn, grad_lat)
    grad_in = dot_nt(grad_q, query_full) + dot_nt(grad_lat, latent_full)
    grad_norm_attn = jnp.sum(grad_in * inputs * scale_attn, axis=0)
    grad_own = grad_in[:rows] + net.flip(grad_in[rows:], 1)
    weighted = grad_own * gain_attn
    own_in, own_scale = inputs[:rows], scale_attn[:rows]
    grad_tokens = (
        grad_residual
        + own_scale * weighted
        - own_in * own_scale**3 * jnp.mean(weighted * own_in, axis=-1, keepdims=True)
    ).astype(bf16)

    def over_chips(value):
        bit = 2
        while bit < R:
            low = value.astype(bf16)
            value = low.astype(f32) + net.flip(low, bit).astype(f32)
            bit <<= 1
        return value.astype(bf16)

    sum_out = over_chips(net.scatter_sum(grad_out_t.reshape(S, part, wide), me))
    sum_kv = over_chips(net.scatter_sum(jnp.concatenate(
        [grad_key_up.reshape(S, lat_rows, wide), grad_value_up.reshape(S, lat_rows, wide)], axis=1), me))
    sum_ql = over_chips(net.scatter_sum(jnp.concatenate(
        [grad_query_w.reshape(S, part, wide), grad_latent_w.reshape(S, part, LAT)], axis=2), me))
    gain_parts = jnp.stack([grad_norm_attn.reshape(S, part), grad_norm_ffn.reshape(S, part)], axis=1)
    sum_gain = over_chips(net.scatter_sum(gain_parts, me))
    sum_gain = sum_gain.astype(f32) + net.flip(sum_gain, 1).astype(f32)

    def both(value, axis):
        other = net.flip(value, 1)
        joined = jnp.where(
            core == 0,
            jnp.concatenate([value, other], axis=axis),
            jnp.concatenate([other, value], axis=axis),
        )
        return joined.astype(f32)

    both_query = both(sum_ql[:, :wide], 1)
    both_latent = both(sum_ql[:, wide:], 1)
    both_kv = both(sum_kv[None], 0)
    both_out = both(sum_out.T, 0)

    def all_reps(value):
        blocks = net.rep_gather(value.astype(bf16))
        full = jnp.zeros((R,) + value.shape, bf16)
        for j, block in enumerate(blocks):
            full = lax.dynamic_update_slice(full, block[None], (rep ^ j, 0, 0))
        return full

    down_w = all_reps(sum_down).reshape(R * sub, D).astype(f32)

    def join_columns(value):
        full = all_reps(value).reshape(R, part, S, sub).transpose(1, 2, 0, 3)
        return full.reshape(part, FF).astype(f32)

    return (
        output,
        grad_tokens,
        sum_gain[0],
        both_query,
        both_latent,
        both_kv[:, :lat_rows],
        both_kv[:, lat_rows:],
        both_out,
        sum_gain[1],
        join_columns(sum_gate),
        join_columns(sum_up),
        down_w,
    )


def solution(mesh):
    net = Net(mesh.shape["rep"], mesh.shape["shard"])

    def body(*args):
        return shards(net, *args)

    return jax.shard_map(
        body,
        mesh=mesh,
        in_specs=(
            P(("rep", "shard"), None),
            P("shard"),
            P("shard", None),
            P("shard", None),
            P(None, "shard", None),
            P(None, "shard", None),
            P(None, "shard"),
            P("shard"),
            P("shard", None),
            P("shard", None),
            P("shard", None),
            P(("rep", "shard"), None),
        ),
        out_specs=(
            P(("rep", "shard"), None),
            P(("rep", "shard"), None),
            P("shard"),
            P("shard", None),
            P("shard", None),
            P(None, "shard", None),
            P(None, "shard", None),
            P(None, "shard"),
            P("shard"),
            P("shard", None),
            P("shard", None),
            P("shard", None),
        ),
        check_vma=False,
    )
```
